32 devices in a mesh: row: 4 (over y, core), col: 8 (over z, x).
Axes of the slice: x: 2, y: 2, z: 4, core: 2. Of those that a mesh axis runs over, the one named last changes fastest.
Arguments:
- fock_blocks: bfloat16 [4096, 4096], P('row', 'col'), as said below
- factor_blocks: bfloat16 [4096, 4096], P('row', 'col'), may hold values from -1.5 to 1.5
- fock_pattern: int32 [32, 32], P('row', 'col'), may hold values from 0 to 1, as said below
- factor_pattern: int32 [32, 32], P('row', 'col'), may hold values from 0 to 1, as said below
- keep_pattern: int32 [32, 32], P('col', 'row'), may hold values from 0 to 1
Outputs:
- transformed: float32 [4096, 4096], P('col', 'row')
The draws below stay inside these ranges and needn't reach their ends.
Inputs may be any that keep to these rules, and one draw needn't show every extreme that they name: fock_blocks is symmetric. fock_pattern is symmetric with ones on its diagonal. factor_pattern is zero below its diagonal and one on it.
All inputs are finite; a program needn't handle non-finite values.
Results may differ from the reference program's by a relative error of at most 0.0029.
Values may be sent and summed in bfloat16 or wider, within the bound.
No kernel may reach another device: no remote copies, remote signals or barrier semaphores. Data moves between devices by JAX's collectives and lax.ppermute only.
A program may use at most 128 MiB of HBM per device.

```python
import jax
import jax.numpy as jnp
from jax import lax

BLOCK = 128
COL_BLOCKS = 4
NBLOCKS = 32
ROW_BLOCKS = 8
ORDER = 4096


def block_grid():
    row_index = lax.broadcasted_iota(jnp.int32, (NBLOCKS, NBLOCKS), 0)
    column_index = lax.broadcasted_iota(jnp.int32, (NBLOCKS, NBLOCKS), 1)
    return (row_index, column_index)


def band_bits(key, near, chance):
    row_index, column_index = block_grid()
    draws = jax.random.randint(key, (NBLOCKS, NBLOCKS), 0, 1000)
    distance = jnp.abs(row_index - column_index)
    return (distance <= near) | (draws < chance)


def pick_index(key, lowest, highest):
    return jax.random.randint(key, (), lowest, highest, dtype=jnp.int32)


def dense_tile(key, tile_rows, tile_columns):
    row_index, column_index = block_grid()
    tile_row = pick_index(jax.random.fold_in(key, 1), 0, NBLOCKS // tile_rows)
    tile_column = pick_index(jax.random.fold_in(key, 2), 0, NBLOCKS // tile_columns)
    return (row_index // tile_rows == tile_row) & (column_index // tile_columns == tile_column)


def dense_lines(key):
    row_index, column_index = block_grid()
    full_row = pick_index(jax.random.fold_in(key, 3), 0, NBLOCKS)
    full_column = pick_index(jax.random.fold_in(key, 4), 0, NBLOCKS)
    return (row_index == full_row) | (column_index == full_column)


def draw_fock_pattern(key, part):
    row_index, column_index = block_grid()
    bits = band_bits(jax.random.fold_in(key, 11), 1, 120)
    mirrored = jnp.where(row_index <= column_index, bits, bits.T)
    marked = dense_tile(jax.random.fold_in(key, 14), ROW_BLOCKS, COL_BLOCKS) | dense_lines(jax.random.fold_in(key, 15))
    return jnp.where(mirrored | marked | marked.T, 1, 0).astype(jnp.int32)


def draw_factor_pattern(key, part):
    row_index, column_index = block_grid()
    bits = band_bits(jax.random.fold_in(key, 12), 1, 150)
    tile_key = jax.random.fold_in(key, 16)
    tile_row = pick_index(jax.random.fold_in(tile_key, 1), 0, NBLOCKS // ROW_BLOCKS - 1)
    lowest_column = ((tile_row + 1) * ROW_BLOCKS + COL_BLOCKS - 1) // COL_BLOCKS
    tile_column = pick_index(jax.random.fold_in(tile_key, 2), lowest_column, NBLOCKS // COL_BLOCKS)
    in_tile = (row_index // ROW_BLOCKS == tile_row) & (column_index // COL_BLOCKS == tile_column)
    full_row = pick_index(jax.random.fold_in(tile_key, 3), 0, ROW_BLOCKS)
    full_column = pick_index(jax.random.fold_in(tile_key, 4), NBLOCKS - COL_BLOCKS, NBLOCKS)
    marked = bits | in_tile | (row_index == full_row) | (column_index == full_column)
    return jnp.where(marked & (row_index <= column_index), 1, 0).astype(jnp.int32)


def draw_keep_pattern(key, part):
    bits = band_bits(jax.random.fold_in(key, 13), 2, 350)
    marked = dense_tile(jax.random.fold_in(key, 17), COL_BLOCKS, ROW_BLOCKS) | dense_lines(jax.random.fold_in(key, 18))
    return jnp.where(bits | marked, 1, 0).astype(jnp.int32)


def draw_fock_blocks(key, part):
    base_key = jax.random.fold_in(key, 21)
    values = jax.random.normal(base_key, (ORDER, ORDER), jnp.float32) * 0.05
    row_index = lax.broadcasted_iota(jnp.int32, (ORDER, ORDER), 0)
    column_index = lax.broadcasted_iota(jnp.int32, (ORDER, ORDER), 1)
    return jnp.where(row_index <= column_index, values, values.T).astype(jnp.bfloat16)


def shard_levels(key, extent, cuts, least, high):
    def one(dim, parts):
        steps = jax.random.uniform(jax.random.fold_in(jax.random.fold_in(key, 6), dim), (parts,), jnp.float32, least / len(cuts), high / len(cuts))
        return jnp.repeat(jnp.exp(steps), extent[dim] // parts).reshape((-1,) + (1,) * (len(extent) - dim - 1))

    level = one(*cuts[0])
    for cut in cuts[1:]:
        level = level * one(*cut)
    return level


def gaussian(own_key, shape, spread, limit, cuts=(), kind=jnp.bfloat16):
    array = spread * jax.random.normal(own_key, shape, jnp.float32)
    if cuts:
        array = array * shard_levels(own_key, shape, cuts, -0.22, 0.18)
    return jnp.clip(array, -limit, limit).astype(kind)


def setup_inputs(seed: int = 0) -> dict:
    key_list = jax.random.split(jax.random.key(seed), 6)
    return {
        "fock_blocks": draw_fock_blocks(jax.random.fold_in(key_list[5], 71), 0),
        "factor_blocks": gaussian(key_list[1], (ORDER, ORDER), 16 ** -0.5, 1.5, ((0, 4), (1, 8))),
        "fock_pattern": draw_fock_pattern(jax.random.fold_in(key_list[5], 71), 0),
        "factor_pattern": draw_factor_pattern(jax.random.fold_in(key_list[5], 71), 0),
        "keep_pattern": draw_keep_pattern(jax.random.fold_in(key_list[5], 71), 0),
    }


def expand(pattern):
    return jnp.repeat(jnp.repeat(pattern, BLOCK, axis=0), BLOCK, axis=1)


def reference(fock_blocks, factor_blocks, fock_pattern, factor_pattern, keep_pattern):
    zero_value = jnp.zeros((), fock_blocks.dtype)
    fock_masked = jnp.where(expand(fock_pattern) > 0, fock_blocks, zero_value)
    row_index = lax.broadcasted_iota(jnp.int32, (ORDER, ORDER), 0)
    column_index = lax.broadcasted_iota(jnp.int32, (ORDER, ORDER), 1)
    factor_masked = jnp.where((expand(factor_pattern) > 0) & (row_index <= column_index), factor_blocks, zero_value)
    product = jnp.dot(factor_masked.T, fock_masked, preferred_element_type=jnp.float32)
    kept = jnp.where(expand(keep_pattern) > 0, product, jnp.zeros((), jnp.float32)).astype(jnp.bfloat16)
    return jnp.dot(kept, factor_masked, preferred_element_type=jnp.float32)
```

```python
import jax
import jax.numpy as jnp
from jax import lax
from jax.sharding import PartitionSpec as P

BLOCK = 128
BOTH = ("row", "col")


def expand(pattern):
    first, second = pattern.shape
    wide = jnp.broadcast_to(pattern[:, None, :, None], (first, BLOCK, second, BLOCK))
    return wide.reshape(first * BLOCK, second * BLOCK)


def dot(left, right, left_dim, right_dim):
    return lax.dot_general(
        left, right, (((left_dim,), (right_dim,)), ((), ())), preferred_element_type=jnp.float32
    )


def make_shards(rows, cols):
    planes = cols // 2
    chips = rows // 2
    places = [(r, z, x) for r in range(rows) for z in range(planes) for x in range(2)]

    def device(r, z, x):
        return r * cols + 2 * z + x

    def move(array, pairs):
        return lax.ppermute(array, BOTH, pairs)

    def holds(r, shift, plane):
        source = r - 2 * shift
        return source >= 0 and 0 <= plane < planes and plane // 2 == r // 2 and source <= plane

    def heading(r):
        return 1 if 2 * (r // 2) < planes // 2 else -1

    x_swap = [(device(r, zz, xx), device(r, zz, 1 - xx)) for r, zz, xx in places]
    core_swap = [(device(r, zz, xx), device(r ^ 1, zz, xx)) for r, zz, xx in places]

    def from_lower(array, shift):
        return move(array, [
            (device(r - 2 * shift, zz, xx), device(r, zz, xx)) for r, zz, xx in places if r >= 2 * shift
        ])

    def shards(fock_blocks, factor_blocks, fock_pattern, factor_pattern, keep_pattern):
        row_count, column_count = fock_blocks.shape
        row_place = lax.axis_index("row")
        column_place = lax.axis_index("col")
        y, k = row_place // 2, row_place % 2
        z, x = column_place // 2, column_place % 2
        way_of = jnp.where(2 * y < planes // 2, 1, -1)
        zero_value = jnp.zeros((), jnp.bfloat16)
        row_index = row_place * row_count + lax.broadcasted_iota(jnp.int32, (row_count, column_count), 0)
        column_index = column_place * column_count + lax.broadcasted_iota(jnp.int32, (row_count, column_count), 1)
        tile = jnp.where(
            (expand(factor_pattern) > 0) & (row_index <= column_index), factor_blocks, zero_value
        )
        fock_masked = jnp.where(expand(fock_pattern) > 0, fock_blocks, zero_value)

        own = {}
        for shift in range(chips):
            start = tile
            if shift:
                start = move(tile, [
                    (device(r - 2 * shift, zz, xx), device(r, zz, xx))
                    for r, zz, xx in places if holds(r, shift, zz)
                ])
            own[shift] = [start]
            for sign in (1, -1):
                moving = start
                for step in range(1, planes):
                    pairs = [
                        (device(r, zz, xx), device(r, zz + sign * heading(r), xx))
                        for r, zz, xx in places
                        if 0 <= zz + sign * heading(r) < planes
                        and holds(r, shift, zz - sign * heading(r) * (step - 1))
                    ]
                    if pairs:
                        moving = move(moving, pairs)
                        own[shift].append(moving)

        fock_other = move(fock_masked, x_swap)
        focks = [(fock_masked, fock_other)]
        for shift in range(1, chips):
            focks.append((from_lower(fock_masked, shift), from_lower(fock_other, shift)))

        def kinds_of(shift):
            for sign in (1, -1):
                for step in range(0 if sign == 1 else 1, planes):
                    if any(
                        0 <= zz - sign * heading(r) * step < planes and holds(r, shift, zz - sign * heading(r) * step)
                        for r, zz, xx in places
                    ):
                        yield sign, step

        def choose(pieces, shift, half):
            chosen = None
            for (sign, step), piece in zip(kinds_of(shift), pieces, strict=True):
                hit = z - sign * way_of * step == 2 * y + half
                chosen = jnp.where(hit, piece, zero_value if chosen is None else chosen)
            return chosen

        panel = {(shift, half, 0): choose(own[shift], shift, half) for shift in range(chips) for half in range(2)}

        first = [[
            sum(dot(panel[s, half, 0], focks[s][cc], 0, 0) for s in range(chips)) for cc in range(2)
        ] for half in range(2)]
        kept_rows = []
        for cc in range(2):
            mine = jnp.where(k == 0, first[0][cc], first[1][cc])
            theirs = jnp.where(k == 0, first[1][cc], first[0][cc])
            kept_rows.append((mine + move(theirs, core_swap)).astype(jnp.bfloat16))
        turned = jnp.concatenate([
            jnp.where(x == 0, kept_rows[0], kept_rows[1]), jnp.where(x == 0, kept_rows[1], kept_rows[0])
        ], axis=1)
        turned = move(turned, [(device(r, zz, xx), device(zz, r, xx)) for r, zz, xx in places])

        for shift in range(chips):
            others = [
                move(piece, [
                    (device(r, zz, xx), device(r, zz, 1 - xx))
                    for r, zz, xx in places if holds(r, shift, zz - sign * heading(r) * step)
                ])
                for (sign, step), piece in zip(kinds_of(shift), own[shift], strict=True)
            ]
            for half in range(2):
                panel[shift, half, 1] = choose(others, shift, half)

        kept = jnp.where(expand(keep_pattern) > 0, turned, zero_value)
        kept_cols = [kept] + [from_lower(kept, shift) for shift in range(1, chips)]

        outs = []
        for other in range(2):
            second = [
                sum(dot(kept_cols[s], panel[s, half, other], 1, 0) for s in range(chips)) for half in range(2)
            ]
            mine = jnp.where(k == 0, second[0], second[1])
            theirs = jnp.where(k == 0, second[1], second[0])
            outs.append(mine + move(theirs, core_swap))
        low = jnp.where(x == 0, outs[0], outs[1])
        high = jnp.where(x == 0, outs[1], outs[0])
        return jnp.concatenate([low, high], axis=1)

    return shards


def solution(mesh):
    shards = make_shards(mesh.shape["row"], mesh.shape["col"])
    in_specs = (P("row", "col"), P("row", "col"), P("row", "col"), P("row", "col"), P("col", "row"))
    return jax.shard_map(shards, mesh=mesh, in_specs=in_specs, out_specs=P("col", "row"), check_vma=False)
```
